512 devices in a mesh: dp: 8 (over x, z_hi), expert: 64 (over y, z_lo, core).
Axes of the slice: x: 4, y: 4, z: 16 (z_hi: 2, z_lo: 8; z = z_hi * 8 + z_lo), core: 2. Of those that a mesh axis runs over, the one named last changes fastest.
Arguments:
- tokens: bfloat16 [2, 4096, 2048], P(None, 'expert', 'dp'), may hold values from -6 to 6
- cotangent: bfloat16 [2, 4096, 2048], P(None, 'expert', 'dp'), may hold values from -6 to 6
- routes: int32 [2, 4096, 2], P(None, 'expert'), may hold values from 0 to 63, all different within a row; in each aligned block of 64 rows (0 to 63, 64 to 127, ..., all dimensions but the last counted through in order) at most 3 rows name the same one
- gates: float32 [2, 4096, 2], P(None, 'expert'), may hold values from 0.25 to 1
- source: int32 [64], replicated, may hold values from 0 to 63, as said below
- w_gate_up: bfloat16 [64, 2048, 2, 1024], P('expert', None, None, 'dp'), may hold values from -0.125 to 0.125
- w_down: bfloat16 [64, 1024, 2048], P('expert', 'dp'), may hold values from -0.1875 to 0.1875
- moment_first: bfloat16 [64, 1024, 2048], P('expert', 'dp'), may hold values from -6 to 6
- moment_second: bfloat16 [64, 1024, 2048], P('expert', 'dp'), may hold values from 0.25 to 4
Outputs:
- layer_out: bfloat16 [2, 4096, 2048], P(None, 'expert', 'dp')
- token_grad: bfloat16 [2, 4096, 2048], P(None, 'expert', 'dp')
- update_dir: bfloat16 [64, 1024, 2048], P('expert', 'dp')
- new_first: bfloat16 [64, 1024, 2048], P('expert', 'dp')
- new_second: bfloat16 [64, 1024, 2048], P('expert', 'dp')
The draws below stay inside these ranges and needn't reach their ends.
Inputs may be any that keep to these rules, and one draw needn't show every extreme that they name: `routes`: in each micro-batch, the 64 tokens of one index of expert name no expert more than 3 times, a bound that some block reaches. source[source[s]] = s for every slot; 32 slots take another slot's expert.
All inputs are finite; a program needn't handle non-finite values.
Results may differ from the reference program's by a relative error of at most 0.018.
Values may be sent and summed in bfloat16 or wider, within the bound.
A program may use at most 64 MiB of HBM per device.

```python
import math
import jax
import jax.numpy as jnp
import numpy as np
from jax import lax

D = 2048
FF = 1024
TOP = 2
MB = 2
TOK_MB = 64
EXPERTS = 64
TOKENS = 4096
CAP = 3
N_DP = 8


def draw_source(key, part):
    order = jax.random.permutation(key, EXPERTS).astype(jnp.int32)
    pair_count = EXPERTS // 4
    first_half = order[0:2 * pair_count:2]
    second = order[1:2 * pair_count:2]
    mapping = jnp.arange(EXPERTS, dtype=jnp.int32)
    mapping = mapping.at[first_half].set(second).at[second].set(first_half)
    return mapping


def shard_levels(rng, shape, pieces, low, largest):
    level, own = 1.0, jax.random.fold_in(rng, 6)
    for dim, blocks in pieces:
        heights = jnp.exp(jax.random.uniform(jax.random.fold_in(own, dim), (blocks,), jnp.float32, low / len(pieces), largest / len(pieces)))
        level = level * jnp.repeat(heights, shape[dim] // blocks).reshape([-1 if axis == dim else 1 for axis in range(len(shape))])
    return level


def shared_out(own_key, own, number, rows, amount, top, most, skew):
    ranking = jax.random.permutation(own_key, amount)
    heavy_load, ordinary = shares(amount, rows * top, most, skew, True), shares(amount, rows * top, most, skew, False)
    places = jnp.arange(amount)

    def named(lengths, offset_by):
        used = int((lengths > 0).sum())
        fixed = max(1, used // 4)
        shifted = fixed + (places - fixed + offset_by * (used - fixed)) % max(1, amount - fixed)
        return jnp.zeros((amount,), jnp.int32).at[ranking[jnp.where(places < fixed, places, shifted)]].set(jnp.asarray(lengths, jnp.int32))

    lengths = jnp.where(number % 4 == 0, named(heavy_load, number // 4), named(ordinary, number - number // 4 - 1))
    mixed = jax.random.permutation(jax.random.fold_in(own, 3), amount)
    source_of, sink = mixed[0:amount // 2 * 2:2], mixed[1:amount // 2 * 2:2]
    room = jnp.minimum(lengths[source_of] - 1, most - lengths[sink]) // 2
    room = jnp.where((source_of == ranking[0]) | (sink == ranking[0]) | (lengths[sink] == 0), 0, jnp.maximum(room, 0))
    shifted = jax.random.randint(jax.random.fold_in(own, 4), (amount // 2,), 0, 1 << 20) % (room + 1)
    lengths = lengths.at[source_of].add(-shifted).at[sink].add(shifted)
    members = jnp.searchsorted(jnp.cumsum(lengths), jnp.arange(rows * top), side="right").astype(jnp.int32)
    grid = members.reshape(top, rows).T
    grid = grid[jax.random.permutation(jax.random.fold_in(own, 1), rows)]
    offset_by = jax.random.randint(jax.random.fold_in(own, 2), (rows, 1), 0, top)
    return jnp.take_along_axis(grid, (jnp.arange(top)[None, :] + offset_by) % top, axis=1)


def shares(count, total, limit, lean, full):
    weights = [(1 << 20) // math.isqrt(rank ** lean) + 1 for rank in range(1, count + 1)]
    largest = limit if full else min(limit, max(-(-total // count), total * weights[0] // sum(weights)))
    least = 1 if total - largest >= count - 1 else 0
    holding, rest = [largest] + [least] * (count - 1), total - largest - least * (count - 1)
    while rest > 0:
        candidates = [i for i in range(1, count) if holding[i] < largest] or [i for i in range(1, count) if holding[i] < limit]
        whole, budget = sum([weights[i] for i in candidates]), rest
        for i in candidates:
            extra = min(limit - holding[i], max(1, budget * weights[i] // whole), rest)
            holding[i] = holding[i] + extra
            rest = rest - extra
    return np.array(holding)


def gaussian(stream_key, extent, spread, most, shards=(), held_as=jnp.bfloat16):
    entries = spread * jax.random.normal(stream_key, extent, jnp.float32)
    if shards:
        entries = entries * shard_levels(stream_key, extent, shards, -0.22, 0.18)
    return jnp.clip(entries, -most, most).astype(held_as)


def setup_inputs(seed: int = 0) -> dict:
    streams_of = jax.random.split(jax.random.key(seed), 10)
    tokens = gaussian(streams_of[0], (MB, TOKENS, D), 1.0, 6.0, ((1, 64), (2, 8)))
    cotangent = gaussian(streams_of[1], (MB, TOKENS, D), 1.0, 6.0, ((1, 64), (2, 8)))
    routes_keys = jax.random.split(jax.random.fold_in(streams_of[2], 1), MB * TOKENS // TOK_MB)
    routes_turns = jax.random.permutation(jax.random.fold_in(streams_of[2], 3), MB * TOKENS // TOK_MB)
    routes = jax.vmap(lambda own, number: shared_out(jax.random.fold_in(streams_of[2], 2), own, number, TOK_MB, EXPERTS, TOP, CAP, 2))(routes_keys, routes_turns).reshape((MB, TOKENS, TOP))
    gates = jnp.clip(0.25 + 0.75 * jax.random.uniform(streams_of[3], (MB, TOKENS, TOP), jnp.float32) ** shard_levels(streams_of[3], (MB, TOKENS, TOP), ((1, 64),), -0.2, 0.2), 0.25, 1.0)
    source = draw_source(jax.random.fold_in(streams_of[9], 71), 0)
    w_gate_up = gaussian(streams_of[5], (EXPERTS, D, 2, FF), D ** -0.5, 0.125, ((0, 64), (3, 8)))
    w_down = gaussian(streams_of[6], (EXPERTS, FF, D), FF ** -0.5, 0.1875, ((0, 64), (1, 8)))
    moment_first = gaussian(streams_of[7], (EXPERTS, FF, D), 1.0, 6.0, ((0, 64), (1, 8)))
    moment_second = jnp.clip(jnp.exp(math.log(4.0) - 2.7725887 * jax.random.uniform(streams_of[8], (EXPERTS, FF, D), jnp.float32) ** shard_levels(streams_of[8], (EXPERTS, FF, D), ((0, 64), (1, 8)), -0.2, 0.2)), 0.25, 4.0).astype(jnp.bfloat16)
    return dict(tokens=tokens, cotangent=cotangent, routes=routes, gates=gates, source=source, w_gate_up=w_gate_up, w_down=w_down, moment_first=moment_first, moment_second=moment_second)


def expert_pass(inputs):
    row_tokens, row_grads, gate_up, down, moment_one, moment_two = inputs
    group_width = FF // N_DP
    down_grad = jnp.zeros((FF, D), jnp.float32)
    outputs = []
    input_grads = []
    gate_up_flat = gate_up.reshape(D, 2 * FF)
    for micro in range(MB):
        expert_in = row_tokens[micro]
        grad_in = row_grads[micro]
        both = jnp.dot(expert_in, gate_up_flat, preferred_element_type=jnp.float32).reshape(-1, 2, FF)
        gate_pre = both[:, 0]
        up_pre = both[:, 1]
        gate_sig = jax.nn.sigmoid(gate_pre)
        hidden = (gate_pre * gate_sig * up_pre).astype(jnp.bfloat16)
        partial_out = jnp.einsum('rgf,gfd->grd', hidden.reshape(-1, N_DP, group_width).astype(jnp.float32), down.reshape(N_DP, group_width, D).astype(jnp.float32))
        partial_out = lax.optimization_barrier(partial_out.astype(jnp.bfloat16)).astype(jnp.float32)
        outputs.append(lax.optimization_barrier(jnp.sum(partial_out, axis=0)).astype(jnp.bfloat16))
        hidden_grad = jnp.dot(grad_in, down.T, preferred_element_type=jnp.float32)
        down_grad = down_grad + jnp.dot(hidden.T, grad_in, preferred_element_type=jnp.float32)
        gate_grad = hidden_grad * up_pre * gate_sig * (1.0 + gate_pre * (1.0 - gate_sig))
        up_grad = hidden_grad * gate_pre * gate_sig
        both_grad = jnp.stack([gate_grad, up_grad], axis=1).astype(jnp.bfloat16)
        partial_in = jnp.einsum('rcgf,dcgf->grd', both_grad.reshape(-1, 2, N_DP, group_width).astype(jnp.float32), gate_up.reshape(D, 2, N_DP, group_width).astype(jnp.float32))
        partial_in = lax.optimization_barrier(partial_in.astype(jnp.bfloat16)).astype(jnp.float32)
        input_grads.append(lax.optimization_barrier(jnp.sum(partial_in, axis=0)).astype(jnp.bfloat16))
    first = 0.9 * moment_one.astype(jnp.float32) + 0.1 * down_grad
    second = 0.999 * moment_two.astype(jnp.float32) + 0.001 * down_grad * down_grad
    update = first / (jnp.sqrt(second) + 1e-08)
    return (jnp.stack(outputs), jnp.stack(input_grads), update.astype(jnp.bfloat16), first.astype(jnp.bfloat16), second.astype(jnp.bfloat16))

def reference(tokens, cotangent, routes, gates, source, w_gate_up, w_down, moment_first, moment_second):
    pair_rows = TOK_MB * TOP
    target = source[routes]
    blocks = target.reshape(MB, EXPERTS, pair_rows)
    onehot = (blocks[..., None] == jnp.arange(EXPERTS, dtype=jnp.int32)).astype(jnp.int32)
    position = lax.optimization_barrier(jnp.sum((jnp.cumsum(onehot, axis=2) - onehot) * onehot, axis=-1)).astype(jnp.int32)
    source_idx = jnp.arange(EXPERTS, dtype=jnp.int32)[None, :, None]
    micro_idx = jnp.arange(MB, dtype=jnp.int32)[:, None, None]
    token_rep = jnp.repeat(tokens.reshape(MB, EXPERTS, TOK_MB, D), TOP, axis=2)
    gate_flat = gates.reshape(MB, EXPERTS, pair_rows)
    grad_rep = (jnp.repeat(cotangent.reshape(MB, EXPERTS, TOK_MB, D).astype(jnp.float32), TOP, axis=2) * gate_flat[..., None]).astype(jnp.bfloat16)
    empty = jnp.zeros((MB, EXPERTS, EXPERTS, CAP, D), jnp.bfloat16)
    token_buf = empty.at[micro_idx, blocks, source_idx, position].set(token_rep)
    grad_buf = empty.at[micro_idx, blocks, source_idx, position].set(grad_rep)
    token_buf = jnp.transpose(token_buf.reshape(MB, EXPERTS, EXPERTS * CAP, D), (1, 0, 2, 3))
    grad_buf = jnp.transpose(grad_buf.reshape(MB, EXPERTS, EXPERTS * CAP, D), (1, 0, 2, 3))
    expert_out, rows_grad, update_dir, new_first, new_second = lax.map(expert_pass, (token_buf, grad_buf, w_gate_up[source], w_down[source], moment_first[source], moment_second[source]))
    expert_out = expert_out.reshape(EXPERTS, MB, EXPERTS, CAP, D)
    rows_grad = rows_grad.reshape(EXPERTS, MB, EXPERTS, CAP, D)
    picked_out = expert_out[blocks, micro_idx, source_idx, position].astype(jnp.float32)
    picked_grad = rows_grad[blocks, micro_idx, source_idx, position].astype(jnp.float32)
    picked_out = picked_out.reshape(MB, EXPERTS, TOK_MB, TOP, D) * gates.reshape(MB, EXPERTS, TOK_MB, TOP)[..., None]
    layer_out = lax.optimization_barrier(jnp.sum(picked_out, axis=3)).astype(jnp.bfloat16).reshape(MB, TOKENS, D)
    token_grad = lax.optimization_barrier(jnp.sum(picked_grad.reshape(MB, EXPERTS, TOK_MB, TOP, D), axis=3)).astype(jnp.bfloat16).reshape(MB, TOKENS, D)
    return (layer_out, token_grad, update_dir, new_first, new_second)
```

```python
import functools

import jax
import jax.numpy as jnp
from jax import lax
from jax.experimental import pallas as pl
from jax.experimental.pallas import tpu as pltpu
from jax.sharding import PartitionSpec as P

MESH = pl.DeviceIdType.MESH
CAP = 3
NX = 4
first_first = (((0,), (0,)), ((), ()))
last_last = (((1,), (1,)), ((), ()))


def mm(a, b, dims=(((1,), (0,)), ((), ()))):
    return lax.dot_general(a, b, dims, preferred_element_type=jnp.float32)


def expert_kernel(
    x_ref, wgu_ref, wd_ref, y_ref, dg_ref,
    full, part, came, zout, zin, acc, dacc, hid, gate_s, up_s,
    z_send, z_recv, x_send, x_recv, own_sem, r_send, r_recv, q_send, q_recv,
):
    width = x_ref.shape[2]
    chunks = x_ref.shape[0]
    dp = lax.axis_index("dp")
    x, zh = dp // 2, dp % 2
    other = x * 2 + (1 - zh)
    peers = [((x + k) % NX) * 2 + zh for k in range(1, NX)]

    def cols(index, size):
        return pl.ds(pl.multiple_of(index * size, size), size)

    barrier = pltpu.get_barrier_semaphore()
    for dev in peers + [other]:
        pl.semaphore_signal(barrier, inc=1, device_id={"dp": dev}, device_id_type=MESH)
    pl.semaphore_wait(barrier, NX)

    def remote(src, dst, send, recv, dev):
        return pltpu.make_async_remote_copy(
            src_ref=src, dst_ref=dst, send_sem=send, recv_sem=recv,
            device_id={"dp": dev}, device_id_type=MESH,
        )

    zc, xc, oc = [], [], []
    for c in range(chunks):
        mine = full.at[c, :, cols(dp, width)]
        cp = remote(x_ref.at[c], mine, z_send.at[c], z_recv.at[c], other)
        cp.start()
        zc.append(cp)
        row = []
        for k, dev in enumerate(peers):
            cp = remote(x_ref.at[c], mine, x_send.at[c, 0, k], x_recv.at[c, 0, k], dev)
            cp.start()
            row.append(cp)
        xc.append(row)
        cp = pltpu.make_async_copy(x_ref.at[c], mine, own_sem.at[c])
        cp.start()
        oc.append(cp)
    for c in range(chunks):
        zc[c].wait_recv()
        theirs = full.at[c, :, cols(other, width)]
        for k, dev in enumerate(peers):
            cp = remote(theirs, theirs, x_send.at[c, 1, k], x_recv.at[c, 1, k], dev)
            cp.start()
            xc[c].append(cp)

    rc, qc = [None] * chunks, [None] * chunks

    def arrive(c):
        oc[c].wait()
        for cp in xc[c]:
            cp.wait_recv()

    def scatter(c):
        rc[c] = []
        for k in range(1, NX):
            to = (x + k) % NX
            cp = remote(
                part.at[c, :, cols(to, 2 * width)], came.at[c, k - 1],
                r_send.at[c, k - 1], r_recv.at[c, k - 1], peers[k - 1],
            )
            cp.start()
            rc[c].append(cp)

    def reduce_x(c):
        for cp in rc[c]:
            cp.wait_recv()
        for half in range(2):
            here = part[c, :, cols(x * 2 + half, width)].astype(jnp.float32)
            for k in range(NX - 1):
                here = here + came[c, k, :, half * width:(half + 1) * width].astype(jnp.float32)
            acc[c, half] = here
        zout[c] = acc[c, 1 - zh].astype(jnp.bfloat16)
        qc[c] = remote(zout.at[c], zin.at[c], q_send.at[c], q_recv.at[c], other)
        qc[c].start()

    def forward(m):
        c = 2 * m
        arrive(c)
        both = mm(full[c], wgu_ref[...])
        hidden_part = both.shape[1] // 2
        gate, up = both[:, :hidden_part], both[:, hidden_part:]
        gate_s[m] = gate
        up_s[m] = up
        hid[m] = (gate * (1.0 / (1.0 + jnp.exp(-gate))) * up).astype(jnp.bfloat16)
        part[c] = mm(hid[m], wd_ref[...]).astype(jnp.bfloat16)
        scatter(c)

    def backward(m):
        c = 2 * m + 1
        arrive(c)
        gate, up = gate_s[m], up_s[m]
        sig = 1.0 / (1.0 + jnp.exp(-gate))
        hidden_grad = mm(full[c], wd_ref[...], last_last)
        gate_grad = hidden_grad * up * sig * (1.0 + gate * (1.0 - sig))
        up_grad = hidden_grad * gate * sig
        both_grad = jnp.concatenate([gate_grad, up_grad], axis=1).astype(jnp.bfloat16)
        part[c] = mm(both_grad, wgu_ref[...], last_last).astype(jnp.bfloat16)
        scatter(c)
        dgrad = mm(hid[m], full[c], first_first)
        if m == 0:
            dacc[...] = dgrad
        else:
            dg_ref[...] = (dacc[...] + dgrad).astype(jnp.bfloat16)

    forward(0)
    backward(0)
    reduce_x(0)
    forward(1)
    reduce_x(1)
    backward(1)
    reduce_x(2)
    reduce_x(3)
    for c in range(chunks):
        qc[c].wait_recv()
        y_ref[c] = (acc[c, zh] + zin[c].astype(jnp.float32)).astype(jnp.bfloat16)
    for c in range(chunks):
        zc[c].wait_send()
        qc[c].wait_send()
        for cp in xc[c] + rc[c]:
            cp.wait_send()


def expert_call(x, wgu, wd):
    chunks, rows, width = x.shape
    model, hidden2 = wgu.shape
    hidden = hidden2 // 2
    bf, f32 = jnp.bfloat16, jnp.float32
    dma = pltpu.SemaphoreType.DMA
    flops = 2 * rows * model * hidden * 2 * 7
    vmem = pl.BlockSpec(memory_space=pltpu.VMEM)
    return pl.pallas_call(
        expert_kernel,
        out_shape=(
            jax.ShapeDtypeStruct((chunks, rows, width), bf),
            jax.ShapeDtypeStruct((hidden, model), bf),
        ),
        in_specs=[vmem] * 3,
        out_specs=(vmem, vmem),
        scratch_shapes=[
            pltpu.VMEM((chunks, rows, model), bf),
            pltpu.VMEM((chunks, rows, model), bf),
            pltpu.VMEM((chunks, NX - 1, rows, 2 * width), bf),
            pltpu.VMEM((chunks, rows, width), bf),
            pltpu.VMEM((chunks, rows, width), bf),
            pltpu.VMEM((chunks, 2, rows, width), f32),
            pltpu.VMEM((hidden, model), f32),
            pltpu.VMEM((2, rows, hidden), bf),
            pltpu.VMEM((2, rows, hidden), f32),
            pltpu.VMEM((2, rows, hidden), f32),
            dma((chunks,)), dma((chunks,)),
            dma((chunks, 2, NX - 1)), dma((chunks, 2, NX - 1)),
            dma((chunks,)),
            dma((chunks, NX - 1)), dma((chunks, NX - 1)),
            dma((chunks,)), dma((chunks,)),
        ],
        compiler_params=pltpu.CompilerParams(
            collective_id=0, has_side_effects=True, vmem_limit_bytes=40 << 20
        ),
        cost_estimate=pl.CostEstimate(flops=flops, bytes_accessed=200 << 20, transcendentals=0),
        name="expert",
    )(x, wgu, wd)


def swap_over(value):
    return lax.all_to_all(value, "expert", split_axis=0, concat_axis=0, tiled=True)


def relocate(flat, source):
    return swap_over(jnp.take(swap_over(flat), source, axis=0))


def per_device(
    tokens, cotangent, routes, gates, source, w_gate_up, w_down, moment_first, moment_second
):
    experts = lax.axis_size("expert")
    micro, count, width = tokens.shape
    model = w_gate_up.shape[1]
    hidden = w_gate_up.shape[3]
    top = routes.shape[2]
    slots = experts * CAP
    bf, f32 = jnp.bfloat16, jnp.float32

    chosen = routes.reshape(micro, count * top)
    earlier = jnp.tri(count * top, k=-1, dtype=bool)
    position = jnp.sum(
        ((chosen[:, :, None] == chosen[:, None, :]) & earlier).astype(jnp.int32), axis=2
    )
    slot_of = (chosen * CAP + position).reshape(micro, count, top)
    slot_ids = jnp.arange(slots, dtype=jnp.int32)
    match = slot_of[..., None] == slot_ids
    picks = match.astype(bf)
    plain = jnp.any(match, axis=2).astype(bf)
    slot_gate = jnp.sum(jnp.where(match, gates[..., None], 0.0), axis=(1, 2))

    rows = []
    for m in range(micro):
        rows.append(mm(plain[m], tokens[m], first_first).astype(bf))
        rows.append((mm(plain[m], cotangent[m], first_first) * slot_gate[m][:, None]).astype(bf))
    send = jnp.stack([r.reshape(experts, CAP, width) for r in rows], axis=1)
    arrived = swap_over(send)
    x = jnp.transpose(arrived, (1, 0, 2, 3)).reshape(2 * micro, slots, width)

    wgu = w_gate_up.reshape(model, 2 * hidden)
    wd = w_down.reshape(hidden, model)
    y, dg = expert_call(x, wgu, wd)

    back = jnp.transpose(y.reshape(2 * micro, experts, CAP, width), (1, 0, 2, 3))
    ret = jnp.transpose(swap_over(back), (1, 0, 2, 3)).reshape(2 * micro, slots, width)
    layer_out, token_grad = [], []
    for m in range(micro):
        out = jnp.zeros((count, width), f32)
        grad = jnp.zeros((count, width), f32)
        for k in range(top):
            out = out + gates[m][:, k:k + 1] * mm(picks[m, :, k], ret[2 * m])
            grad = grad + mm(picks[m, :, k], ret[2 * m + 1])
        layer_out.append(out.astype(bf))
        token_grad.append(grad.astype(bf))

    shares = (experts, hidden // experts, model)
    moments = jnp.concatenate([moment_first.reshape(shares), moment_second.reshape(shares)], axis=1)
    moments = relocate(moments, source)
    down_grad = relocate(dg.reshape(shares), source).reshape(hidden, model).astype(f32)
    half = hidden // experts
    first = 0.9 * moments[:, :half].reshape(hidden, model).astype(f32) + 0.1 * down_grad
    second = (
        0.999 * moments[:, half:].reshape(hidden, model).astype(f32)
        + 0.001 * down_grad * down_grad
    )
    update = first / (jnp.sqrt(second) + 1e-08)
    shape = moment_first.shape
    return (
        jnp.stack(layer_out),
        jnp.stack(token_grad),
        update.astype(bf).reshape(shape),
        first.astype(bf).reshape(shape),
        second.astype(bf).reshape(shape),
    )


def solution(mesh):
    placed = (
        P(None, "expert", "dp"),
        P(None, "expert", "dp"),
        P(None, "expert", None),
        P(None, "expert", None),
        P(),
        P("expert", None, None, "dp"),
        P("expert", "dp", None),
        P("expert", "dp", None),
        P("expert", "dp", None),
    )
    return jax.shard_map(
        per_device,
        mesh=mesh,
        in_specs=placed,
        out_specs=(
            P(None, "expert", "dp"),
            P(None, "expert", "dp"),
            P("expert", "dp", None),
            P("expert", "dp", None),
            P("expert", "dp", None),
        ),
        check_vma=False,
    )
```
